512 devices in a mesh: lat: 16 (over z_hi, x), lev: 32 (over y, z_lo, core).
Axes of the slice: x: 4, y: 8, z: 8 (z_hi: 4, z_lo: 2; z = z_hi * 2 + z_lo), core: 2. Of those that a mesh axis runs over, the one named last changes fastest.
Arguments:
- state: float32 [6, 48, 128, 1152], P(None, 'lat', 'lev'), may hold values from -6 to 6
- courant: float32 [2, 48, 128, 1152], P(None, 'lat', 'lev'), may hold values from -0.4 to 0.4
- offsets: int32 [2, 48, 128, 1152], P(None, 'lat', 'lev'), may hold values from -1 to 2
- log_thickness: float32 [48, 128, 1152], P('lat', 'lev'), may hold values from 0.05 to 0.5
- surface: float32 [48, 1152], P('lat'), may hold values from -6 to 6
- remap_level: int32 [48, 128, 1152], P('lat', None, 'lev'), may hold values from 0 to 127, as said below
- remap_weight: float32 [48, 128, 1152], P('lat', None, 'lev'), may hold values from 0 to 1
Outputs:
- remapped: float32 [6, 48, 128, 1152], P(None, 'lat', 'lev')
- geopotential: float32 [48, 128, 1152], P('lat', 'lev')
The draws below stay inside these ranges and needn't reach their ends.
Inputs may be any that keep to these rules, and one draw needn't show every extreme that they name: `remap_level`: the source level of target level k lies within 2 of k.
All inputs are finite; a program needn't handle non-finite values.
Results may differ from the reference program's by a relative error of at most 0.00007.
Values sent between devices are 32-bit elements; how exact they have to be, the bound alone decides.
No kernel may reach another device: no remote copies, remote signals or barrier semaphores. Data moves between devices by JAX's collectives and lax.ppermute only.
A program may use at most 64 MiB of HBM per device.

```python
import math
import jax
import jax.numpy as jnp
from jax import lax

NLON = 1152
SUBSTEPS = 2
FIELDS = 6
NLAT = 48
LEV = 128


def draw_remap_level(key, part):
    spread = jax.random.randint(key, (NLAT, LEV, NLON), -2, 3, dtype=jnp.int32)
    levels = jnp.arange(LEV, dtype=jnp.int32)[None, :, None]
    return jnp.clip(levels + spread, 0, LEV - 1).astype(jnp.int32)


def place_ends(array, stream_key, least, top_value):
    extent = array.shape
    index_at = [jax.random.randint(jax.random.fold_in(stream_key, axis), (), 0, extent[axis]) for axis in range(len(extent))]
    array = array.at[tuple(index_at)].set(least)
    longest = extent.index(max(extent))
    index_at[longest] = (index_at[longest] + 1) % extent[longest]
    return array.at[tuple(index_at)].set(top_value)


def level_of(own_key, extent, shards, smallest, largest):
    def one(axis_at, shards_of):
        steps = jax.random.uniform(jax.random.fold_in(jax.random.fold_in(own_key, 6), axis_at), (shards_of,), jnp.float32, smallest / len(shards), largest / len(shards))
        return jnp.repeat(jnp.exp(steps), extent[axis_at] // shards_of).reshape((-1,) + (1,) * (len(extent) - axis_at - 1))

    factor_of = one(*shards[0])
    for cut in shards[1:]:
        factor_of = factor_of * one(*cut)
    return factor_of


def gaussian(stream_key, shape, scale, most, pieces=(), kind=jnp.bfloat16):
    result = jax.random.normal(stream_key, shape, jnp.float32) * scale
    if len(pieces) > 0:
        result = level_of(stream_key, shape, pieces, -0.22, 0.18) * result
    return jnp.clip(result, min=-most, max=most).astype(kind)


def setup_inputs(seed: int = 0) -> dict:
    key_list = jax.random.split(jax.random.key(seed), 8)
    state = gaussian(key_list[0], (FIELDS, NLAT, LEV, NLON), 1.0, 6.0, ((1, 16), (2, 32)), jnp.float32)
    courant = jnp.clip(jax.random.uniform(key_list[1], (2, NLAT, LEV, NLON), jnp.float32, -0.4, 0.4) * level_of(key_list[1], (2, NLAT, LEV, NLON), ((1, 16), (2, 32)), -0.4, 0.0), -0.4, 0.4)
    offsets = place_ends(jax.random.randint(key_list[2], (2, NLAT, LEV, NLON), -1, 3), jax.random.fold_in(key_list[2], 1), -1, 2).astype(jnp.int32)
    log_thickness = jnp.clip(jnp.exp(math.log(0.5) - 2.3025851 * jax.random.uniform(key_list[3], (NLAT, LEV, NLON), jnp.float32) ** level_of(key_list[3], (NLAT, LEV, NLON), ((0, 16), (1, 32)), -0.2, 0.2)), 0.05, 0.5)
    surface = gaussian(key_list[4], (NLAT, NLON), 1.0, 6.0, ((0, 16),), jnp.float32)
    remap_level = draw_remap_level(jax.random.fold_in(key_list[7], 71), 0)
    remap_weight = jnp.clip(1.0 * jax.random.uniform(key_list[6], (NLAT, LEV, NLON), jnp.float32) ** level_of(key_list[6], (NLAT, LEV, NLON), ((0, 16), (2, 32)), -0.2, 0.2), 0.0, 1.0)
    return {"state": state, "courant": courant, "offsets": offsets, "log_thickness": log_thickness, "surface": surface, "remap_level": remap_level, "remap_weight": remap_weight}


def parabola(q, source, weight):
    n = q.shape[-2]
    widths = [(0, 0)] * (q.ndim - 2) + [(2, 2), (0, 0)]
    padded = jnp.pad(q, widths, mode="edge")
    edges = (7.0 * (padded[..., 1:n + 2, :] + padded[..., 2:n + 3, :]) - (padded[..., 0:n + 1, :] + padded[..., 3:n + 4, :])) / 12.0
    centre = jnp.take_along_axis(q, source, axis=-2)
    left = jnp.take_along_axis(edges[..., :n, :], source, axis=-2)
    right = jnp.take_along_axis(edges[..., 1:, :], source, axis=-2)
    slope = right - left
    curve = 6.0 * centre - 3.0 * (left + right)
    return left + weight * (slope + curve * (1.0 - weight))


def reference(state, courant, offsets, log_thickness, surface, remap_level, remap_weight):
    rows = state.shape[1]
    width = state.shape[3]
    row_index = jnp.arange(rows, dtype=jnp.int32)[:, None, None]
    north_index = row_index + offsets[0] + 2
    east_index = (jnp.arange(width, dtype=jnp.int32)[None, None, :] + offsets[1]) % width

    def advect(q):
        for substep in range(SUBSTEPS):
            padded = jnp.pad(q, ((2, 2), (0, 0), (0, 0)))
            north = courant[0] * jnp.take_along_axis(padded, north_index, axis=0)
            south = jnp.concatenate([jnp.zeros_like(north[:1]), north[:-1]], axis=0)
            east = courant[1] * jnp.take_along_axis(q, east_index, axis=2)
            west = jnp.roll(east, 1, axis=2)
            q = q - (north - south) - (east - west)
        return q

    advected = lax.map(advect, state)
    heating = advected[0] * log_thickness
    lower = jnp.cumsum(heating[:, ::-1], axis=1)[:, ::-1] - heating
    geopotential = surface[:, None, :] + lower + 0.5 * heating
    remapped = lax.map(lambda q: parabola(q, remap_level, remap_weight), advected)
    return remapped, geopotential
```

```python
import functools

import jax
import jax.numpy as jnp
from jax import lax
from jax.experimental import pallas as pl
from jax.experimental.pallas import tpu as pltpu
from jax.sharding import PartitionSpec as P


def pick(offset, behind, here, ahead, beyond):
    return jnp.where(
        offset == -1,
        behind,
        jnp.where(offset == 0, here, jnp.where(offset == 1, ahead, beyond)),
    )


def east_kernel(q_ref, courant_ref, offsets_ref, base_ref):
    count, rows, _, width = q_ref.shape
    for row in range(rows):
        offset = offsets_ref[1, row]
        weight = courant_ref[1, row]
        for f in range(count):
            q = q_ref[f, row]
            moved = pick(
                offset,
                pltpu.roll(q, 1, 1),
                q,
                pltpu.roll(q, width - 1, 1),
                pltpu.roll(q, width - 2, 1),
            )
            east = weight * moved
            base_ref[f, row] = q - (east - pltpu.roll(east, 1, 1))


def advected(f, base_ref, q_ref, low_ref, high_ref, face_ref, courant_ref, offsets_ref):
    rows = q_ref.shape[1]
    around = (
        [low_ref[f, 0], low_ref[f, 1]]
        + [q_ref[f, row] for row in range(rows)]
        + [high_ref[f, 0], high_ref[f, 1]]
    )
    south = face_ref[6, 0] * pick(face_ref[6, 1].astype(jnp.int32), *around[0:4])
    result = []
    for row in range(rows):
        north = courant_ref[0, row] * pick(offsets_ref[0, row], *around[row + 1 : row + 5])
        result.append(base_ref[f, row] - (north - south))
        south = north
    return result


def first_kernel(base_ref, q_ref, low_ref, high_ref, courant_ref, offsets_ref, out_ref, up_ref, down_ref):
    count, rows = q_ref.shape[:2]
    for f in range(count):
        new = advected(f, base_ref, q_ref, low_ref, high_ref, low_ref, courant_ref, offsets_ref)
        for row in range(rows):
            out_ref[f, row] = new[row]
        for k in range(2):
            up_ref[f, k] = new[rows - 2 + k]
            down_ref[f, k] = new[k]


def second_kernel(
    base_ref,
    q_ref,
    low_ref,
    high_ref,
    face_ref,
    courant_ref,
    offsets_ref,
    thickness_ref,
    surface_ref,
    out_ref,
    part_ref,
    sums_ref,
):
    count, rows, levels, width = q_ref.shape
    sums = []
    for f in range(count):
        new = advected(f, base_ref, q_ref, low_ref, high_ref, face_ref, courant_ref, offsets_ref)
        for row in range(rows):
            out_ref[f, row] = new[row]
            if f == 0:
                heating = new[row] * thickness_ref[row]
                below = jnp.zeros((1, width), jnp.float32)
                deeper = []
                for k in range(levels - 1, -1, -1):
                    deeper.insert(0, below)
                    below = below + heating[k : k + 1]
                part_ref[row] = (
                    jnp.concatenate(deeper, axis=0) + 0.5 * heating + surface_ref[row : row + 1]
                )
                sums.append(below)
    sums = jnp.concatenate(sums, axis=0)
    for k in range(sums_ref.shape[0]):
        sums_ref[k] = sums


def remap_kernel(q_ref, above_ref, under_ref, delta_ref, weight_ref, out_ref):
    count, rows, levels, width = q_ref.shape
    me = lax.axis_index("lev")
    is_first = me == 0
    is_last = me == lax.axis_size("lev") - 1
    sub = lax.broadcasted_iota(jnp.int32, (8, width), 0)
    for row in range(rows):
        delta = delta_ref[row].astype(jnp.int32)
        source = jnp.concatenate([delta, delta], axis=0) + (sub & 3) + 2
        t = weight_ref[row]
        for f in range(count):
            own = q_ref[f, row]
            above = jnp.where(is_first, jnp.broadcast_to(own[0:1], own.shape), above_ref[f, row])
            under = jnp.where(is_last, jnp.broadcast_to(own[levels - 1 :], own.shape), under_ref[f, row])
            early = jnp.concatenate([above, own], axis=0)
            late = jnp.concatenate([own, under], axis=0)
            windows = [early]
            for k in range(1, 4):
                windows.append(
                    jnp.where(sub < 4, pltpu.roll(early, 8 - k, 0), pltpu.roll(late, 4 - k, 0))
                )
            windows.append(late)
            w0, w1, w2, w3, w4 = windows
            left = (7.0 * (w1 + w2) - (w0 + w3)) * (1.0 / 12.0)
            right = (7.0 * (w2 + w3) - (w1 + w4)) * (1.0 / 12.0)
            slope = right - left
            curve = 6.0 * w2 - 3.0 * (left + right)
            left, slope, curve = (
                jnp.take_along_axis(x, source, axis=0)[:levels] for x in (left, slope, curve)
            )
            out_ref[f, row] = left + t * (slope + curve * (1.0 - t))


def close_kernel(part_ref, sums_ref, out_ref):
    rows = part_ref.shape[0]
    me = lax.axis_index("lev")
    total = jnp.zeros(sums_ref.shape[1:], jnp.float32)
    for k in range(sums_ref.shape[0]):
        total = total + jnp.where(k > me, sums_ref[k], 0.0)
    for row in range(rows):
        out_ref[row] = part_ref[row] + total[row : row + 1]


def call(kernel, out, flops, *args):
    shapes = [jax.ShapeDtypeStruct(s, jnp.float32) for s in out]
    size = sum(x.size for x in args) + sum(s.size for s in shapes)
    return pl.pallas_call(
        kernel,
        out_shape=shapes,
        in_specs=[pl.BlockSpec(memory_space=pltpu.VMEM)] * len(args),
        out_specs=[pl.BlockSpec(memory_space=pltpu.VMEM)] * len(out),
        cost_estimate=pl.CostEstimate(flops=flops, bytes_accessed=4 * size, transcendentals=0),
    )(*args)


def per_device(state, courant, offsets, log_thickness, surface, remap_level, remap_weight):
    count, rows, levels, width = state.shape
    lats, groups = lax.axis_size("lat"), lax.axis_size("lev")

    def ahead(n):
        return [(i, i + 1) for i in range(n - 1)]

    def back(n):
        return [(i + 1, i) for i in range(n - 1)]

    work = 20 * state.size
    face = jnp.stack([courant[0, rows - 1], offsets[0, rows - 1].astype(jnp.float32)])
    up = jnp.concatenate([state[:, rows - 2 :], face[None]], axis=0)
    low = lax.ppermute(up, "lat", ahead(lats))
    high = lax.ppermute(state[:, :2], "lat", back(lats))

    total_levels = remap_level.shape[1]
    delta_col = (remap_level - jnp.arange(total_levels, dtype=jnp.int32)[None, :, None]).astype(
        jnp.float32
    )
    inputs = lax.all_to_all(
        jnp.stack([delta_col, remap_weight]), "lev", split_axis=2, concat_axis=3, tiled=True
    )

    (base,) = call(east_kernel, [state.shape], work, state, courant, offsets)
    edge = (count, 2, levels, width)
    field, up, down = call(
        first_kernel, [state.shape, edge, edge], work, base, state, low, high, courant, offsets
    )
    low2 = lax.ppermute(up, "lat", ahead(lats))
    high2 = lax.ppermute(down, "lat", back(lats))
    (base,) = call(east_kernel, [state.shape], work, field, courant, offsets)
    field, part, sums = call(
        second_kernel,
        [state.shape, log_thickness.shape, (groups, rows, width)],
        work,
        base,
        field,
        low2,
        high2,
        low,
        courant,
        offsets,
        log_thickness,
        surface,
    )
    above = lax.ppermute(field, "lev", ahead(groups))
    under = lax.ppermute(field, "lev", back(groups))
    sums = lax.all_to_all(sums, "lev", 0, 0, tiled=True)
    (remapped,) = call(
        remap_kernel, [state.shape], 2 * work, field, above, under, inputs[0], inputs[1]
    )
    (geopotential,) = call(close_kernel, [log_thickness.shape], sums.size, part, sums)
    return (remapped, geopotential)


def solution(mesh):
    in_specs = (
        P(None, "lat", "lev", None),
        P(None, "lat", "lev", None),
        P(None, "lat", "lev", None),
        P("lat", "lev", None),
        P("lat", None),
        P("lat", None, "lev"),
        P("lat", None, "lev"),
    )
    out_specs = (P(None, "lat", "lev", None), P("lat", "lev", None))
    return jax.shard_map(
        per_device, mesh=mesh, in_specs=in_specs, out_specs=out_specs, check_vma=False
    )
```

```python
import jax
import jax.numpy as jnp
from jax import lax
from jax.experimental import pallas as pl
from jax.experimental.pallas import tpu as pltpu
from jax.sharding import PartitionSpec as P


NEAR = 4


def pick(offset, behind, here, ahead, beyond):
    return jnp.where(
        offset == -1,
        behind,
        jnp.where(offset == 0, here, jnp.where(offset == 1, ahead, beyond)),
    )


def east_kernel(q_ref, courant_ref, offsets_ref, base_ref):
    count, rows, _, width = q_ref.shape
    for row in range(rows):
        offset = offsets_ref[1, row]
        weight = courant_ref[1, row]
        for f in range(count):
            q = q_ref[f, row]
            moved = pick(
                offset,
                pltpu.roll(q, 1, 1),
                q,
                pltpu.roll(q, width - 1, 1),
                pltpu.roll(q, width - 2, 1),
            )
            east = weight * moved
            base_ref[f, row] = q - (east - pltpu.roll(east, 1, 1))


def is_even():
    return lax.rem(lax.axis_index("lat"), 2) == 0


def advected(f, base_ref, q_ref, slow_ref, fast_ref, face, courant_ref, offsets_ref):
    rows = q_ref.shape[1]
    even = is_even()
    low, high = [], []
    for k in range(2):
        slow, fast = slow_ref[f, k], fast_ref[f, k]
        low.append(jnp.where(even, slow, fast))
        high.append(jnp.where(even, fast, slow))
    around = low + [q_ref[f, row] for row in range(rows)] + high
    south = face[0] * pick(face[1], *around[0:4])
    result = []
    for row in range(rows):
        north = courant_ref[0, row] * pick(offsets_ref[0, row], *around[row + 1 : row + 5])
        result.append(base_ref[f, row] - (north - south))
        south = north
    return result


def send(f, new, slow_ref, fast_ref):
    even = is_even()
    for k in range(2):
        up, down = new[len(new) - 2 + k], new[k]
        slow_ref[f, k] = jnp.where(even, down, up)
        fast_ref[f, k] = jnp.where(even, up, down)


def edges_kernel(q_ref, courant_ref, offsets_ref, slow_ref, fast_ref):
    count, rows = q_ref.shape[:2]
    for f in range(count):
        send(f, [q_ref[f, row] for row in range(rows)], slow_ref, fast_ref)
    for k, value in enumerate((courant_ref[0, rows - 1], offsets_ref[0, rows - 1].astype(jnp.float32))):
        slow_ref[count, k] = value
        fast_ref[count, k] = value


def first_kernel(
    base_ref, q_ref, slow_ref, fast_ref, courant_ref, offsets_ref, out_ref, face_ref, next_slow_ref, next_fast_ref
):
    count, rows = q_ref.shape[:2]
    face = [jnp.where(is_even(), slow_ref[count, k], fast_ref[count, k]) for k in range(2)]
    for k in range(2):
        face_ref[k] = face[k]
    face[1] = face[1].astype(jnp.int32)
    for f in range(count):
        new = advected(f, base_ref, q_ref, slow_ref, fast_ref, face, courant_ref, offsets_ref)
        for row in range(rows):
            out_ref[f, row] = new[row]
        send(f, new, next_slow_ref, next_fast_ref)


def heat(new, thickness_ref, surface_ref, part_ref, sums_ref):
    sums = []
    for row, value in enumerate(new):
        levels, width = value.shape
        heating = value * thickness_ref[row]
        below = jnp.zeros((1, width), jnp.float32)
        deeper = []
        for k in range(levels - 1, -1, -1):
            deeper.insert(0, below)
            below = below + heating[k : k + 1]
        part_ref[row] = jnp.concatenate(deeper, axis=0) + 0.5 * heating + surface_ref[row : row + 1]
        sums.append(below)
    sums = jnp.concatenate(sums, axis=0)
    for k in range(sums_ref.shape[0]):
        sums_ref[k] = sums


def second_kernel(
    base_ref, q_ref, slow_ref, fast_ref, face_ref, courant_ref, offsets_ref, thickness_ref, surface_ref,
    out_ref, part_ref, sums_ref,
):
    count, rows = q_ref.shape[:2]
    face = face_ref[0], face_ref[1].astype(jnp.int32)
    for f in range(count):
        new = advected(f, base_ref, q_ref, slow_ref, fast_ref, face, courant_ref, offsets_ref)
        for row in range(rows):
            out_ref[f, row] = new[row]
        if f == 0:
            heat(new, thickness_ref, surface_ref, part_ref, sums_ref)


def remap_kernel(q_ref, chip_ref, other_ref, delta_ref, weight_ref, out_ref):
    count, rows, levels, width = q_ref.shape
    me = lax.axis_index("lev")
    is_first = me == 0
    even = lax.rem(me, 2) == 0
    is_last = me == lax.axis_size("lev") - 1
    sub = lax.broadcasted_iota(jnp.int32, (8, width), 0)
    for row in range(rows):
        delta = delta_ref[row].astype(jnp.int32)
        source = jnp.concatenate([delta, delta], axis=0) + (sub & 3) + 2
        t = weight_ref[row]
        for f in range(count):
            own = q_ref[f, row]
            above, under = chip_ref[f, row], other_ref[f, row]
            above, under = jnp.where(even, under, above), jnp.where(even, above, under)
            above = jnp.where(is_first, jnp.broadcast_to(own[0:1], own.shape), above)
            under = jnp.where(is_last, jnp.broadcast_to(own[levels - 1 :], own.shape), under)
            early = jnp.concatenate([above, own], axis=0)
            late = jnp.concatenate([own, under], axis=0)
            windows = [early]
            for k in range(1, 4):
                windows.append(
                    jnp.where(sub < 4, pltpu.roll(early, 8 - k, 0), pltpu.roll(late, 4 - k, 0))
                )
            windows.append(late)
            w0, w1, w2, w3, w4 = windows
            left = (7.0 * (w1 + w2) - (w0 + w3)) * (1.0 / 12.0)
            right = (7.0 * (w2 + w3) - (w1 + w4)) * (1.0 / 12.0)
            slope = right - left
            curve = 6.0 * w2 - 3.0 * (left + right)
            left, slope, curve = (
                jnp.take_along_axis(x, source, axis=0)[:levels] for x in (left, slope, curve)
            )
            out_ref[f, row] = left + t * (slope + curve * (1.0 - t))


def columns_kernel(level_ref, weight_ref, out_ref, held):
    rows, width, total = level_ref.shape
    at = lax.broadcasted_iota(jnp.int32, (width, total), 1)
    held[...] = jnp.zeros_like(held)
    for row in range(rows):
        held[row * width : (row + 1) * width] = (level_ref[row] - at).astype(jnp.float32)
        start = (rows + row) * width
        held[start : start + width] = weight_ref[row]
    turned = held[...].T
    count, levels, _ = out_ref.shape
    for k in range(count):
        out_ref[k] = turned[k * levels : (k + 1) * levels]


def join_kernel(in_ref, delta_ref, weight_ref):
    count = in_ref.shape[0]
    rows = delta_ref.shape[0]
    width = delta_ref.shape[2] // count
    for k in range(count):
        to = k * width
        for row in range(rows):
            delta_ref[row, :, to : to + width] = in_ref[k, :, row * width : (row + 1) * width]
            start = (rows + row) * width
            weight_ref[row, :, to : to + width] = in_ref[k, :, start : start + width]


def group_kernel(sums_ref, own_ref, out_ref):
    near = sums_ref.shape[0]
    me = lax.rem(lax.axis_index("lev"), near)
    own = jnp.zeros(sums_ref.shape[1:], jnp.float32)
    total = own
    for k in range(near):
        own = own + jnp.where(k > me, sums_ref[k], 0.0)
        total = total + sums_ref[k]
    own_ref[...] = own
    for k in range(out_ref.shape[0]):
        out_ref[k] = total


def close_kernel(part_ref, own_ref, sums_ref, out_ref):
    rows = part_ref.shape[0]
    me = lax.axis_index("lev") // NEAR
    total = own_ref[...]
    for k in range(sums_ref.shape[0]):
        total = total + jnp.where(k > me, sums_ref[k], 0.0)
    for row in range(rows):
        out_ref[row] = part_ref[row] + total[row : row + 1]


def call(kernel, out, flops, *args, scratch=()):
    shapes = [jax.ShapeDtypeStruct(s, jnp.float32) for s in out]
    size = sum(x.size for x in args) + sum(s.size for s in shapes)
    return pl.pallas_call(
        kernel,
        out_shape=shapes,
        scratch_shapes=scratch,
        in_specs=[pl.BlockSpec(memory_space=pltpu.VMEM)] * len(args),
        out_specs=[pl.BlockSpec(memory_space=pltpu.VMEM)] * len(out),
        compiler_params=pltpu.CompilerParams(vmem_limit_bytes=16 << 20),
        cost_estimate=pl.CostEstimate(flops=flops, bytes_accessed=4 * size, transcendentals=0),
    )(*args)


def per_device(state, courant, offsets, log_thickness, surface, remap_level, remap_weight):
    count, rows, levels, width = state.shape
    lats, groups = lax.axis_size("lat"), lax.axis_size("lev")

    def swaps(n, first):
        return [p for i in range(first, n - 1, 2) for p in ((i, i + 1), (i + 1, i))]

    work = 20 * state.size
    edge = (count, 2, levels, width)
    slow, fast = call(
        edges_kernel, [(count + 1, *edge[1:])] * 2, 1, state, courant, offsets
    )
    slow = lax.ppermute(slow, "lat", swaps(lats, 1))
    fast = lax.ppermute(fast, "lat", swaps(lats, 0))
    far = groups // NEAR
    close = [[j * NEAR + i for i in range(NEAR)] for j in range(far)]
    distant = [[j * NEAR + i for j in range(far)] for i in range(NEAR)]

    def exchange(x, among):
        return lax.all_to_all(x, "lev", 0, 0, tiled=True, axis_index_groups=among)

    (columns,) = call(
        columns_kernel,
        [(groups, levels, 256)],
        remap_level.size,
        jnp.transpose(remap_level, (0, 2, 1)),
        jnp.transpose(remap_weight, (0, 2, 1)),
        scratch=[pltpu.VMEM((256, remap_level.shape[1]), jnp.float32)],
    )
    columns = lax.all_to_all(columns, "lev", 0, 0, tiled=True)

    (base,) = call(east_kernel, [state.shape], work, state, courant, offsets)
    field, face, slow, fast = call(
        first_kernel, [state.shape, (2, levels, width), edge, edge], work, base, state, slow, fast, courant, offsets
    )
    slow = lax.ppermute(slow, "lat", swaps(lats, 1))
    fast = lax.ppermute(fast, "lat", swaps(lats, 0))
    (base,) = call(east_kernel, [state.shape], work, field, courant, offsets)
    delta, weight = call(join_kernel, [log_thickness.shape] * 2, columns.size, columns)
    delta, weight = call(join_kernel, [log_thickness.shape] * 2, columns.size, columns)
    field, part, sums = call(
        second_kernel, [state.shape, log_thickness.shape, (NEAR, rows, width)], work, base, field, slow, fast, face,
        courant, offsets, log_thickness, surface,
    )
    sums = exchange(sums, close)
    own, sums = call(group_kernel, [(rows, width), (far, rows, width)], sums.size, sums)
    above = lax.ppermute(field, "lev", swaps(groups, 0))
    under = lax.ppermute(field, "lev", swaps(groups, 1))
    sums = exchange(sums, distant)
    (remapped,) = call(
        remap_kernel, [state.shape], 2 * work, field, above, under, delta, weight
    )
    (geopotential,) = call(close_kernel, [log_thickness.shape], sums.size, part, own, sums)
    return (remapped, geopotential)


def solution(mesh):
    in_specs = (
        P(None, "lat", "lev", None),
        P(None, "lat", "lev", None),
        P(None, "lat", "lev", None),
        P("lat", "lev", None),
        P("lat", None),
        P("lat", None, "lev"),
        P("lat", None, "lev"),
    )
    out_specs = (P(None, "lat", "lev", None), P("lat", "lev", None))

    return jax.shard_map(per_device, mesh=mesh, in_specs=in_specs, out_specs=out_specs, check_vma=False)
```

```python
import jax
import jax.numpy as jnp
from jax import lax
from jax.experimental import pallas as pl
from jax.experimental.pallas import tpu as pltpu
from jax.sharding import PartitionSpec as P


NEAR = 4


def pick(offset, behind, here, ahead, beyond):
    return jnp.where(
        offset == -1,
        behind,
        jnp.where(offset == 0, here, jnp.where(offset == 1, ahead, beyond)),
    )


def east_kernel(q_ref, courant_ref, offsets_ref, base_ref):
    count, rows, _, width = q_ref.shape
    for row in range(rows):
        offset = offsets_ref[1, row]
        weight = courant_ref[1, row]
        for f in range(count):
            q = q_ref[f, row]
            moved = pick(
                offset,
                pltpu.roll(q, 1, 1),
                q,
                pltpu.roll(q, width - 1, 1),
                pltpu.roll(q, width - 2, 1),
            )
            east = weight * moved
            base_ref[f, row] = q - (east - pltpu.roll(east, 1, 1))


def is_even():
    return lax.rem(lax.axis_index("lat"), 2) == 0


def advected(f, base_ref, q_ref, slow_ref, fast_ref, face, courant_ref, offsets_ref):
    rows = q_ref.shape[1]
    even = is_even()
    low, high = [], []
    for k in range(2):
        slow, fast = slow_ref[f, k], fast_ref[f, k]
        low.append(jnp.where(even, slow, fast))
        high.append(jnp.where(even, fast, slow))
    around = low + [q_ref[f, row] for row in range(rows)] + high
    south = face[0] * pick(face[1], *around[0:4])
    result = []
    for row in range(rows):
        north = courant_ref[0, row] * pick(offsets_ref[0, row], *around[row + 1 : row + 5])
        result.append(base_ref[f, row] - (north - south))
        south = north
    return result


def send(f, new, slow_ref, fast_ref):
    even = is_even()
    for k in range(2):
        up, down = new[len(new) - 2 + k], new[k]
        slow_ref[f, k] = jnp.where(even, down, up)
        fast_ref[f, k] = jnp.where(even, up, down)


def edges_kernel(q_ref, courant_ref, offsets_ref, slow_ref, fast_ref, held, sems):
    count, rows = q_ref.shape[:2]
    even = is_even()
    up, down = rows - 2, 0
    copies = [
        pltpu.make_async_copy(
            q_ref.at[:, pl.ds(jnp.where(even, down, up), 2)], slow_ref.at[0:count], sems.at[0]
        ),
        pltpu.make_async_copy(
            q_ref.at[:, pl.ds(jnp.where(even, up, down), 2)], fast_ref.at[0:count], sems.at[1]
        ),
        pltpu.make_async_copy(courant_ref.at[0, rows - 1], slow_ref.at[count, 0], sems.at[2]),
        pltpu.make_async_copy(courant_ref.at[0, rows - 1], fast_ref.at[count, 0], sems.at[3]),
        pltpu.make_async_copy(offsets_ref.at[0, rows - 1], held, sems.at[4]),
    ]
    for copy in copies:
        copy.start()
    copies[4].wait()
    offset = held[...].astype(jnp.float32)
    slow_ref[count, 1] = offset
    fast_ref[count, 1] = offset
    for copy in copies[:4]:
        copy.wait()


def first_kernel(
    base_ref, q_ref, slow_ref, fast_ref, courant_ref, offsets_ref, out_ref, face_ref, next_slow_ref, next_fast_ref
):
    count, rows = q_ref.shape[:2]
    face = [jnp.where(is_even(), slow_ref[count, k], fast_ref[count, k]) for k in range(2)]
    for k in range(2):
        face_ref[k] = face[k]
    face[1] = face[1].astype(jnp.int32)
    for f in range(count):
        new = advected(f, base_ref, q_ref, slow_ref, fast_ref, face, courant_ref, offsets_ref)
        for row in range(rows):
            out_ref[f, row] = new[row]
        send(f, new, next_slow_ref, next_fast_ref)


def heat(new, thickness_ref, surface_ref, part_ref, sums_ref):
    sums = []
    for row, value in enumerate(new):
        levels, width = value.shape
        heating = value * thickness_ref[row]
        below = jnp.zeros((1, width), jnp.float32)
        deeper = []
        for k in range(levels - 1, -1, -1):
            deeper.insert(0, below)
            below = below + heating[k : k + 1]
        part_ref[row] = jnp.concatenate(deeper, axis=0) + 0.5 * heating + surface_ref[row : row + 1]
        sums.append(below)
    sums = jnp.concatenate(sums, axis=0)
    for k in range(sums_ref.shape[0]):
        sums_ref[k] = sums


def second_kernel(
    base_ref, q_ref, slow_ref, fast_ref, face_ref, courant_ref, offsets_ref, thickness_ref, surface_ref,
    out_ref, part_ref, sums_ref,
):
    count, rows = q_ref.shape[:2]
    face = face_ref[0], face_ref[1].astype(jnp.int32)
    for f in range(count):
        new = advected(f, base_ref, q_ref, slow_ref, fast_ref, face, courant_ref, offsets_ref)
        for row in range(rows):
            out_ref[f, row] = new[row]
        if f == 0:
            heat(new, thickness_ref, surface_ref, part_ref, sums_ref)


def remap_kernel(q_ref, chip_ref, other_ref, delta_ref, weight_ref, out_ref):
    count, rows, levels, width = q_ref.shape
    me = lax.axis_index("lev")
    is_first = me == 0
    even = lax.rem(me, 2) == 0
    is_last = me == lax.axis_size("lev") - 1
    sub = lax.broadcasted_iota(jnp.int32, (8, width), 0)
    for row in range(rows):
        delta = delta_ref[row].astype(jnp.int32)
        source = jnp.concatenate([delta, delta], axis=0) + (sub & 3) + 2
        t = weight_ref[row]
        for f in range(count):
            own = q_ref[f, row]
            above, under = chip_ref[f, row], other_ref[f, row]
            above, under = jnp.where(even, under, above), jnp.where(even, above, under)
            above = jnp.where(is_first, jnp.broadcast_to(own[0:1], own.shape), above)
            under = jnp.where(is_last, jnp.broadcast_to(own[levels - 1 :], own.shape), under)
            early = jnp.concatenate([above, own], axis=0)
            late = jnp.concatenate([own, under], axis=0)
            windows = [early]
            for k in range(1, 4):
                windows.append(
                    jnp.where(sub < 4, pltpu.roll(early, 8 - k, 0), pltpu.roll(late, 4 - k, 0))
                )
            windows.append(late)
            w0, w1, w2, w3, w4 = windows
            left = (7.0 * (w1 + w2) - (w0 + w3)) * (1.0 / 12.0)
            right = (7.0 * (w2 + w3) - (w1 + w4)) * (1.0 / 12.0)
            slope = right - left
            curve = 6.0 * w2 - 3.0 * (left + right)
            left, slope, curve = (
                jnp.take_along_axis(x, source, axis=0)[:levels] for x in (left, slope, curve)
            )
            out_ref[f, row] = left + t * (slope + curve * (1.0 - t))


def columns_kernel(level_ref, weight_ref, out_ref, held):
    rows, width, total = level_ref.shape
    at = lax.broadcasted_iota(jnp.int32, (width, total), 1)
    held[...] = jnp.zeros_like(held)
    for row in range(rows):
        held[row * width : (row + 1) * width] = (level_ref[row] - at).astype(jnp.float32)
        start = (rows + row) * width
        held[start : start + width] = weight_ref[row]
    turned = held[...].T
    count, levels, _ = out_ref.shape
    for k in range(count):
        out_ref[k] = turned[k * levels : (k + 1) * levels]


def join_kernel(in_ref, delta_ref, weight_ref):
    count = in_ref.shape[0]
    rows = delta_ref.shape[0]
    width = delta_ref.shape[2] // count
    for k in range(count):
        to = k * width
        for row in range(rows):
            delta_ref[row, :, to : to + width] = in_ref[k, :, row * width : (row + 1) * width]
            start = (rows + row) * width
            weight_ref[row, :, to : to + width] = in_ref[k, :, start : start + width]


def group_kernel(sums_ref, out_ref):
    near = out_ref.shape[0]
    me = lax.axis_index("lev")
    group, place = me // near, lax.rem(me, near)
    deeper = jnp.zeros(sums_ref.shape[1:], jnp.float32)
    for k in range(sums_ref.shape[0]):
        deeper = deeper + jnp.where(k > group, sums_ref[k], 0.0)
    own = sums_ref[group]
    for k in range(near):
        out_ref[k] = deeper + jnp.where(place > k, own, 0.0)


def close_kernel(part_ref, sums_ref, out_ref):
    total = sums_ref[0]
    for k in range(1, sums_ref.shape[0]):
        total = total + sums_ref[k]
    for row in range(part_ref.shape[0]):
        out_ref[row] = part_ref[row] + total[row : row + 1]


def call(kernel, out, flops, *args, scratch=()):
    shapes = [jax.ShapeDtypeStruct(s, jnp.float32) for s in out]
    size = sum(x.size for x in args) + sum(s.size for s in shapes)
    return pl.pallas_call(
        kernel,
        out_shape=shapes,
        scratch_shapes=scratch,
        in_specs=[pl.BlockSpec(memory_space=pltpu.VMEM)] * len(args),
        out_specs=[pl.BlockSpec(memory_space=pltpu.VMEM)] * len(out),
        compiler_params=pltpu.CompilerParams(vmem_limit_bytes=16 << 20),
        cost_estimate=pl.CostEstimate(flops=flops, bytes_accessed=4 * size, transcendentals=0),
    )(*args)


def per_device(state, courant, offsets, log_thickness, surface, remap_level, remap_weight):
    count, rows, levels, width = state.shape
    lats, groups = lax.axis_size("lat"), lax.axis_size("lev")

    def swaps(n, first):
        return [p for i in range(first, n - 1, 2) for p in ((i, i + 1), (i + 1, i))]

    work = 20 * state.size
    edge = (count, 2, levels, width)
    slow, fast = pl.pallas_call(
        edges_kernel,
        out_shape=[jax.ShapeDtypeStruct((count + 1, *edge[1:]), jnp.float32)] * 2,
        in_specs=[pl.BlockSpec(memory_space=pltpu.HBM)] * 3,
        out_specs=[pl.BlockSpec(memory_space=pltpu.VMEM)] * 2,
        scratch_shapes=[pltpu.VMEM((levels, width), jnp.int32), pltpu.SemaphoreType.DMA((5,))],
        compiler_params=pltpu.CompilerParams(vmem_limit_bytes=16 << 20),
    )(*(pltpu.with_memory_space_constraint(x, pltpu.HBM) for x in (state, courant, offsets)))
    slow = lax.ppermute(slow, "lat", swaps(lats, 1))
    fast = lax.ppermute(fast, "lat", swaps(lats, 0))
    far = groups // NEAR
    close = [[j * NEAR + i for i in range(NEAR)] for j in range(far)]
    distant = [[j * NEAR + i for j in range(far)] for i in range(NEAR)]

    def exchange(x, among):
        return lax.all_to_all(x, "lev", 0, 0, tiled=True, axis_index_groups=among)

    (columns,) = call(
        columns_kernel,
        [(groups, levels, 256)],
        remap_level.size,
        jnp.transpose(remap_level, (0, 2, 1)),
        jnp.transpose(remap_weight, (0, 2, 1)),
        scratch=[pltpu.VMEM((256, remap_level.shape[1]), jnp.float32)],
    )
    columns = lax.all_to_all(columns, "lev", 0, 0, tiled=True)

    (base,) = call(east_kernel, [state.shape], work, state, courant, offsets)
    field, face, slow, fast = call(
        first_kernel, [state.shape, (2, levels, width), edge, edge], work, base, state, slow, fast, courant, offsets
    )
    slow = lax.ppermute(slow, "lat", swaps(lats, 1))
    fast = lax.ppermute(fast, "lat", swaps(lats, 0))
    (base,) = call(east_kernel, [state.shape], work, field, courant, offsets)
    delta, weight = call(join_kernel, [log_thickness.shape] * 2, columns.size, columns)
    delta, weight = call(join_kernel, [log_thickness.shape] * 2, columns.size, columns)
    field, part, sums = call(
        second_kernel, [state.shape, log_thickness.shape, (far, rows, width)], work, base, field, slow, fast, face,
        courant, offsets, log_thickness, surface,
    )
    sums = exchange(sums, distant)
    (sums,) = call(group_kernel, [(NEAR, rows, width)], sums.size, sums)
    above = lax.ppermute(field, "lev", swaps(groups, 0))
    under = lax.ppermute(field, "lev", swaps(groups, 1))
    sums = exchange(sums, close)
    (remapped,) = call(remap_kernel, [state.shape], 2 * work, field, above, under, delta, weight)
    (geopotential,) = call(close_kernel, [log_thickness.shape], sums.size, part, sums)
    return (remapped, geopotential)


def solution(mesh):
    in_specs = (
        P(None, "lat", "lev", None),
        P(None, "lat", "lev", None),
        P(None, "lat", "lev", None),
        P("lat", "lev", None),
        P("lat", None),
        P("lat", None, "lev"),
        P("lat", None, "lev"),
    )
    out_specs = (P(None, "lat", "lev", None), P("lat", "lev", None))

    return jax.shard_map(
        per_device, mesh=mesh, in_specs=in_specs, out_specs=out_specs, check_vma=False
    )
```

```python
import jax
import jax.numpy as jnp
from jax import lax
from jax.experimental import pallas as pl
from jax.experimental.pallas import tpu as pltpu
from jax.sharding import PartitionSpec as P


NEAR = 4


def pick(offset, behind, here, ahead, beyond):
    return jnp.where(
        offset == -1,
        behind,
        jnp.where(offset == 0, here, jnp.where(offset == 1, ahead, beyond)),
    )


def east_kernel(q_ref, courant_ref, offsets_ref, base_ref):
    count, rows, levels, width = q_ref.shape
    for row in range(rows):
        offset = jnp.concatenate([offsets_ref[1, row]] * 2, axis=0)
        weight = jnp.concatenate([courant_ref[1, row]] * 2, axis=0)
        for f in range(0, count, 2):
            q = jnp.concatenate([q_ref[f, row], q_ref[f + 1, row]], axis=0)
            moved = pick(
                offset,
                pltpu.roll(q, 1, 1),
                q,
                pltpu.roll(q, width - 1, 1),
                pltpu.roll(q, width - 2, 1),
            )
            east = weight * moved
            base = q - (east - pltpu.roll(east, 1, 1))
            base_ref[f, row] = base[:levels]
            base_ref[f + 1, row] = base[levels:]


def is_even():
    return lax.rem(lax.axis_index("lat"), 2) == 0


def advected(f, base_ref, q_ref, slow_ref, fast_ref, face, courant_ref, offsets_ref, g=None):
    g = f if g is None else g
    rows = q_ref.shape[1]
    even = is_even()
    low, high = [], []
    for k in range(2):
        slow, fast = slow_ref[g, k], fast_ref[f, k]
        low.append(jnp.where(even, slow, fast))
        high.append(jnp.where(even, fast, slow))
    around = low + [q_ref[f, row] for row in range(rows)] + high
    south = face[0] * pick(face[1], *around[0:4])
    result = []
    for row in range(rows):
        north = courant_ref[0, row] * pick(offsets_ref[0, row], *around[row + 1 : row + 5])
        result.append(base_ref[f, row] - (north - south))
        south = north
    return result


def send(f, new, slow_ref, fast_ref, g=None):
    g = f if g is None else g
    even = is_even()
    for k in range(2):
        up, down = new[len(new) - 2 + k], new[k]
        slow_ref[g, k] = jnp.where(even, down, up)
        fast_ref[f, k] = jnp.where(even, up, down)


def edges_kernel(q_ref, courant_ref, offsets_ref, slow_ref, fast_ref, held, sems):
    count, rows = q_ref.shape[:2]
    even = is_even()
    up, down = rows - 2, 0
    copies = [
        pltpu.make_async_copy(
            q_ref.at[:, pl.ds(jnp.where(even, down, up), 2)], slow_ref.at[0:count], sems.at[0]
        ),
        pltpu.make_async_copy(
            q_ref.at[:, pl.ds(jnp.where(even, up, down), 2)], fast_ref.at[0:count], sems.at[1]
        ),
        pltpu.make_async_copy(courant_ref.at[0, rows - 1], slow_ref.at[count, 0], sems.at[2]),
        pltpu.make_async_copy(courant_ref.at[0, rows - 1], fast_ref.at[count, 0], sems.at[3]),
        pltpu.make_async_copy(offsets_ref.at[0, rows - 1], held, sems.at[4]),
    ]
    for copy in copies:
        copy.start()
    copies[4].wait()
    offset = held[...].astype(jnp.float32)
    slow_ref[count, 1] = offset
    fast_ref[count, 1] = offset
    for copy in copies[:4]:
        copy.wait()


def first_kernel(
    base_ref, q_ref, slow_ref, fast_ref, courant_ref, offsets_ref, out_ref, face_ref, slow0_ref, next_slow_ref,
    next_fast_ref,
):
    count, rows = q_ref.shape[:2]
    face = [jnp.where(is_even(), slow_ref[count, k], fast_ref[count, k]) for k in range(2)]
    for k in range(2):
        face_ref[k] = face[k]
    face[1] = face[1].astype(jnp.int32)
    for f in range(count):
        new = advected(f, base_ref, q_ref, slow_ref, fast_ref, face, courant_ref, offsets_ref)
        for row in range(rows):
            out_ref[f, row] = new[row]
        if f == 0:
            send(0, new, slow0_ref, next_fast_ref)
        else:
            send(f, new, next_slow_ref, next_fast_ref, f - 1)


def heat(new, thickness_ref, surface_ref, part_ref, sums_ref):
    sums = []
    for row, value in enumerate(new):
        levels = value.shape[0]
        heating = value * thickness_ref[row]
        below = jnp.concatenate([heating, jnp.zeros_like(heating)], axis=0)
        step = 1
        while step < levels:
            below = below + pltpu.roll(below, 2 * levels - step, 0)
            step *= 2
        part_ref[row] = below[:levels] - 0.5 * heating + surface_ref[row : row + 1]
        sums.append(below[0:1])
    sums = jnp.concatenate(sums, axis=0)
    for k in range(sums_ref.shape[0]):
        sums_ref[k] = sums


def heat_kernel(
    base_ref, q_ref, slow_ref, fast_ref, face_ref, courant_ref, offsets_ref, thickness_ref, surface_ref,
    out_ref, part_ref, sums_ref,
):
    face = face_ref[0], face_ref[1].astype(jnp.int32)
    new = advected(0, base_ref, q_ref, slow_ref, fast_ref, face, courant_ref, offsets_ref)
    for row, value in enumerate(new):
        out_ref[row] = value
    heat(new, thickness_ref, surface_ref, part_ref, sums_ref)


def second_kernel(
    base_ref, q_ref, slow_ref, fast_ref, face_ref, courant_ref, offsets_ref, done_ref, out_ref
):
    count, rows = q_ref.shape[:2]
    face = face_ref[0], face_ref[1].astype(jnp.int32)
    for row in range(rows):
        out_ref[0, row] = done_ref[row]
    for f in range(1, count):
        new = advected(f, base_ref, q_ref, slow_ref, fast_ref, face, courant_ref, offsets_ref, f - 1)
        for row in range(rows):
            out_ref[f, row] = new[row]


def remap_kernel(q_ref, chip_ref, other_ref, delta_ref, weight_ref, out_ref):
    count, rows, levels, width = q_ref.shape
    me = lax.axis_index("lev")
    is_first = me == 0
    even = lax.rem(me, 2) == 0
    is_last = me == lax.axis_size("lev") - 1
    sub = lax.broadcasted_iota(jnp.int32, (8, width), 0)
    for row in range(rows):
        delta = delta_ref[row].astype(jnp.int32)
        source = jnp.concatenate([delta, delta], axis=0) + (sub & 3) + 2
        t = weight_ref[row]
        for f in range(count):
            own = q_ref[f, row]
            above, under = chip_ref[f, row], other_ref[f, row]
            above, under = jnp.where(even, under, above), jnp.where(even, above, under)
            above = jnp.where(is_first, jnp.broadcast_to(own[0:1], own.shape), above)
            under = jnp.where(is_last, jnp.broadcast_to(own[levels - 1 :], own.shape), under)
            early = jnp.concatenate([above, own], axis=0)
            late = jnp.concatenate([own, under], axis=0)
            windows = [early]
            for k in range(1, 4):
                windows.append(
                    jnp.where(sub < 4, pltpu.roll(early, 8 - k, 0), pltpu.roll(late, 4 - k, 0))
                )
            windows.append(late)
            w0, w1, w2, w3, w4 = windows
            left = (7.0 * (w1 + w2) - (w0 + w3)) * (1.0 / 12.0)
            right = (7.0 * (w2 + w3) - (w1 + w4)) * (1.0 / 12.0)
            slope = right - left
            curve = 6.0 * w2 - 3.0 * (left + right)
            left, slope, curve = (
                jnp.take_along_axis(x, source, axis=0)[:levels] for x in (left, slope, curve)
            )
            out_ref[f, row] = left + t * (slope + curve * (1.0 - t))


def columns_kernel(level_ref, weight_ref, out_ref, held):
    rows, width, total = level_ref.shape
    at = lax.broadcasted_iota(jnp.int32, (width, total), 1)
    held[...] = jnp.zeros_like(held)
    for row in range(rows):
        held[row * width : (row + 1) * width] = (level_ref[row] - at).astype(jnp.float32)
        start = (rows + row) * width
        held[start : start + width] = weight_ref[row]
    turned = held[...].T
    count, levels, _ = out_ref.shape
    for k in range(count):
        out_ref[k] = turned[k * levels : (k + 1) * levels]


def join_kernel(in_ref, delta_ref, weight_ref):
    count = in_ref.shape[0]
    rows = delta_ref.shape[0]
    width = delta_ref.shape[2] // count
    for k in range(count):
        to = k * width
        for row in range(rows):
            delta_ref[row, :, to : to + width] = in_ref[k, :, row * width : (row + 1) * width]
            start = (rows + row) * width
            weight_ref[row, :, to : to + width] = in_ref[k, :, start : start + width]


def group_kernel(sums_ref, out_ref):
    near = out_ref.shape[0]
    me = lax.axis_index("lev")
    group, place = lax.div(me, near), lax.rem(me, near)
    deeper = jnp.zeros(sums_ref.shape[1:], jnp.float32)
    for k in range(sums_ref.shape[0]):
        deeper = deeper + jnp.where(k > group, sums_ref[k], 0.0)
    own = sums_ref[group]
    for k in range(near):
        out_ref[k] = deeper + jnp.where(place > k, own, 0.0)


def close_kernel(part_ref, sums_ref, out_ref):
    total = sums_ref[0]
    for k in range(1, sums_ref.shape[0]):
        total = total + sums_ref[k]
    for row in range(part_ref.shape[0]):
        out_ref[row] = part_ref[row] + total[row : row + 1]


def call(kernel, out, flops, *args, scratch=()):
    shapes = [jax.ShapeDtypeStruct(s, jnp.float32) for s in out]
    size = sum(x.size for x in args) + sum(s.size for s in shapes)
    return pl.pallas_call(
        kernel,
        out_shape=shapes,
        scratch_shapes=scratch,
        in_specs=[pl.BlockSpec(memory_space=pltpu.VMEM)] * len(args),
        out_specs=[pl.BlockSpec(memory_space=pltpu.VMEM)] * len(out),
        compiler_params=pltpu.CompilerParams(vmem_limit_bytes=16 << 20),
        cost_estimate=pl.CostEstimate(flops=flops, bytes_accessed=4 * size, transcendentals=0),
    )(*args)


def per_device(state, courant, offsets, log_thickness, surface, remap_level, remap_weight):
    count, rows, levels, width = state.shape
    lats, groups = lax.axis_size("lat"), lax.axis_size("lev")

    def swaps(n, first):
        return [p for i in range(first, n - 1, 2) for p in ((i, i + 1), (i + 1, i))]

    work = 20 * state.size
    edge = (count, 2, levels, width)
    slow, fast = pl.pallas_call(
        edges_kernel,
        out_shape=[jax.ShapeDtypeStruct((count + 1, *edge[1:]), jnp.float32)] * 2,
        in_specs=[pl.BlockSpec(memory_space=pltpu.HBM)] * 3,
        out_specs=[pl.BlockSpec(memory_space=pltpu.VMEM)] * 2,
        scratch_shapes=[pltpu.VMEM((levels, width), jnp.int32), pltpu.SemaphoreType.DMA((5,))],
        compiler_params=pltpu.CompilerParams(vmem_limit_bytes=16 << 20),
    )(*(pltpu.with_memory_space_constraint(x, pltpu.HBM) for x in (state, courant, offsets)))
    slow = lax.ppermute(slow, "lat", swaps(lats, 1))
    fast = lax.ppermute(fast, "lat", swaps(lats, 0))
    far = groups // NEAR
    close = [[j * NEAR + i for i in range(NEAR)] for j in range(far)]
    distant = [[j * NEAR + i for j in range(far)] for i in range(NEAR)]

    def exchange(x, among):
        return lax.all_to_all(x, "lev", 0, 0, tiled=True, axis_index_groups=among)

    (columns,) = call(
        columns_kernel,
        [(groups, levels, 256)],
        remap_level.size,
        jnp.transpose(remap_level, (0, 2, 1)),
        jnp.transpose(remap_weight, (0, 2, 1)),
        scratch=[pltpu.VMEM((256, remap_level.shape[1]), jnp.float32)],
    )
    columns = lax.all_to_all(columns, "lev", 0, 0, tiled=True)

    (base,) = call(east_kernel, [state.shape], work, state, courant, offsets)
    first, rest = (1, *edge[1:]), (count - 1, *edge[1:])
    field, face, slow0, slow, fast = call(
        first_kernel, [state.shape, (2, levels, width), first, rest, edge], work, base, state, slow, fast,
        courant, offsets,
    )
    slow0 = lax.ppermute(slow0, "lat", swaps(lats, 1))
    fast = lax.ppermute(fast, "lat", swaps(lats, 0))
    slow = lax.ppermute(slow, "lat", swaps(lats, 1))
    (base,) = call(east_kernel, [state.shape], work, field, courant, offsets)
    delta, weight = call(join_kernel, [log_thickness.shape] * 2, columns.size, columns)
    delta, weight = call(join_kernel, [log_thickness.shape] * 2, columns.size, columns)
    done, part, sums = call(
        heat_kernel, [log_thickness.shape, log_thickness.shape, (far, rows, width)], work, base, field, slow0, fast,
        face, courant, offsets, log_thickness, surface,
    )
    (field,) = call(
        second_kernel, [state.shape], work, base, field, slow, fast, face, courant, offsets, done
    )
    sums = exchange(sums, distant)
    (sums,) = call(group_kernel, [(NEAR, rows, width)], sums.size, sums)
    above = lax.ppermute(field, "lev", swaps(groups, 0))
    under = lax.ppermute(field, "lev", swaps(groups, 1))
    sums = exchange(sums, close)
    (remapped,) = call(remap_kernel, [state.shape], 2 * work, field, above, under, delta, weight)
    (geopotential,) = call(close_kernel, [log_thickness.shape], sums.size, part, sums)
    return (remapped, geopotential)


def solution(mesh):
    in_specs = (
        P(None, "lat", "lev", None),
        P(None, "lat", "lev", None),
        P(None, "lat", "lev", None),
        P("lat", "lev", None),
        P("lat", None),
        P("lat", None, "lev"),
        P("lat", None, "lev"),
    )
    out_specs = (P(None, "lat", "lev", None), P("lat", "lev", None))

    return jax.shard_map(
        per_device, mesh=mesh, in_specs=in_specs, out_specs=out_specs, check_vma=False
    )
```

```python
import jax
import jax.numpy as jnp
from jax import lax
from jax.experimental import pallas as pl
from jax.experimental.pallas import tpu as pltpu
from jax.sharding import PartitionSpec as P


NEAR = 4


def pick(offset, behind, here, ahead, beyond):
    return jnp.where(
        offset == -1,
        behind,
        jnp.where(offset == 0, here, jnp.where(offset == 1, ahead, beyond)),
    )


def east_kernel(q_ref, courant_ref, offsets_ref, base_ref):
    count, rows, levels, width = q_ref.shape
    for row in range(rows):
        offset = jnp.concatenate([offsets_ref[1, row]] * 2, axis=0)
        weight = jnp.concatenate([courant_ref[1, row]] * 2, axis=0)
        for f in range(0, count, 2):
            q = jnp.concatenate([q_ref[f, row], q_ref[f + 1, row]], axis=0)
            moved = pick(
                offset,
                pltpu.roll(q, 1, 1),
                q,
                pltpu.roll(q, width - 1, 1),
                pltpu.roll(q, width - 2, 1),
            )
            east = weight * moved
            base = q - (east - pltpu.roll(east, 1, 1))
            base_ref[f, row] = base[:levels]
            base_ref[f + 1, row] = base[levels:]


def is_even():
    return lax.rem(lax.axis_index("lat"), 2) == 0


def advected(f, base_ref, q_ref, slow_ref, fast_ref, face, courant_ref, offsets_ref, g=None):
    g = f if g is None else g
    rows = q_ref.shape[1]
    even = is_even()
    low, high = [], []
    for k in range(2):
        slow, fast = slow_ref[g, k], fast_ref[f, k]
        low.append(jnp.where(even, slow, fast))
        high.append(jnp.where(even, fast, slow))
    around = low + [q_ref[f, row] for row in range(rows)] + high
    south = face[0] * pick(face[1], *around[0:4])
    result = []
    for row in range(rows):
        north = courant_ref[0, row] * pick(offsets_ref[0, row], *around[row + 1 : row + 5])
        result.append(base_ref[f, row] - (north - south))
        south = north
    return result


def send(f, new, slow_ref, fast_ref, g=None):
    g = f if g is None else g
    even = is_even()
    for k in range(2):
        up, down = new[len(new) - 2 + k], new[k]
        slow_ref[g, k] = jnp.where(even, down, up)
        fast_ref[f, k] = jnp.where(even, up, down)


def edges_kernel(q_ref, courant_ref, offsets_ref, slow_ref, fast_ref, held, sems):
    count, rows = q_ref.shape[:2]
    even = is_even()
    up, down = rows - 2, 0
    copies = [
        pltpu.make_async_copy(
            q_ref.at[:, pl.ds(jnp.where(even, down, up), 2)], slow_ref.at[0:count], sems.at[0]
        ),
        pltpu.make_async_copy(
            q_ref.at[:, pl.ds(jnp.where(even, up, down), 2)], fast_ref.at[0:count], sems.at[1]
        ),
        pltpu.make_async_copy(courant_ref.at[0, rows - 1], slow_ref.at[count, 0], sems.at[2]),
        pltpu.make_async_copy(courant_ref.at[0, rows - 1], fast_ref.at[count, 0], sems.at[3]),
        pltpu.make_async_copy(offsets_ref.at[0, rows - 1], held, sems.at[4]),
    ]
    for copy in copies:
        copy.start()
    copies[4].wait()
    offset = held[...].astype(jnp.float32)
    slow_ref[count, 1] = offset
    fast_ref[count, 1] = offset
    for copy in copies[:4]:
        copy.wait()


def first_kernel(
    base_ref, q_ref, slow_ref, fast_ref, courant_ref, offsets_ref, out_ref, face_ref, slow0_ref, next_slow_ref,
    next_fast_ref,
):
    count, rows = q_ref.shape[:2]
    face = [jnp.where(is_even(), slow_ref[count, k], fast_ref[count, k]) for k in range(2)]
    for k in range(2):
        face_ref[k] = face[k]
    face[1] = face[1].astype(jnp.int32)
    for f in range(count):
        new = advected(f, base_ref, q_ref, slow_ref, fast_ref, face, courant_ref, offsets_ref)
        for row in range(rows):
            out_ref[f, row] = new[row]
        if f == 0:
            send(0, new, slow0_ref, next_fast_ref)
        else:
            send(f, new, next_slow_ref, next_fast_ref, f - 1)


def heat(new, thickness_ref, surface_ref, part_ref, sums_ref):
    sums = []
    for row, value in enumerate(new):
        levels = value.shape[0]
        heating = value * thickness_ref[row]
        below = jnp.concatenate([heating, jnp.zeros_like(heating)], axis=0)
        step = 1
        while step < levels:
            below = below + pltpu.roll(below, 2 * levels - step, 0)
            step *= 2
        part_ref[row] = below[:levels] - 0.5 * heating + surface_ref[row : row + 1]
        sums.append(below[0:1])
    sums = jnp.concatenate(sums, axis=1)
    for k in range(sums_ref.shape[0]):
        sums_ref[k] = sums


def heat_kernel(
    base_ref, q_ref, slow_ref, fast_ref, face_ref, courant_ref, offsets_ref, thickness_ref, surface_ref,
    out_ref, part_ref, sums_ref,
):
    face = face_ref[0], face_ref[1].astype(jnp.int32)
    new = advected(0, base_ref, q_ref, slow_ref, fast_ref, face, courant_ref, offsets_ref)
    for row, value in enumerate(new):
        out_ref[row] = value
    heat(new, thickness_ref, surface_ref, part_ref, sums_ref)


def second_kernel(
    base_ref, q_ref, slow_ref, fast_ref, face_ref, courant_ref, offsets_ref, done_ref, out_ref
):
    count, rows = q_ref.shape[:2]
    face = face_ref[0], face_ref[1].astype(jnp.int32)
    for row in range(rows):
        out_ref[0, row] = done_ref[row]
    for f in range(1, count):
        new = advected(f, base_ref, q_ref, slow_ref, fast_ref, face, courant_ref, offsets_ref, f - 1)
        for row in range(rows):
            out_ref[f, row] = new[row]


def remap_kernel(q_ref, chip_ref, other_ref, delta_ref, weight_ref, out_ref):
    count, rows, levels, width = q_ref.shape
    me, last = lax.axis_index("lev"), lax.axis_size("lev") - 1
    even = lax.rem(me, 2) == 0

    def body(above_ref, under_ref):
        sub = lax.broadcasted_iota(jnp.int32, (8, width), 0)
        for row in range(rows):
            delta = delta_ref[row].astype(jnp.int32)
            source = jnp.concatenate([delta, delta], axis=0) + (sub & 3) + 2
            t = weight_ref[row]
            for f in range(count):
                own = q_ref[f, row]
                if above_ref is None:
                    above = jnp.broadcast_to(own[0:1], own.shape)
                else:
                    above = above_ref[f, row]
                if under_ref is None:
                    under = jnp.broadcast_to(own[levels - 1 :], own.shape)
                else:
                    under = under_ref[f, row]
                early = jnp.concatenate([above, own], axis=0)
                late = jnp.concatenate([own, under], axis=0)
                windows = [early]
                for k in range(1, 4):
                    windows.append(
                        jnp.where(sub < 4, pltpu.roll(early, 8 - k, 0), pltpu.roll(late, 4 - k, 0))
                    )
                windows.append(late)
                w0, w1, w2, w3, w4 = windows
                left = 7.0 * (w1 + w2) - (w0 + w3)
                right = 7.0 * (w2 + w3) - (w1 + w4)
                slope = right - left
                curve = 6.0 * w2 - 0.25 * (left + right)
                left, slope, curve = (
                    jnp.take_along_axis(x, source, axis=0)[:levels] for x in (left, slope, curve)
                )
                out_ref[f, row] = (left + t * slope) * (1.0 / 12.0) + t * (1.0 - t) * curve

    pl.when(even & (me > 0))(lambda: body(other_ref, chip_ref))
    pl.when(~even & (me < last))(lambda: body(chip_ref, other_ref))
    pl.when(me == 0)(lambda: body(None, chip_ref))
    pl.when(me == last)(lambda: body(chip_ref, None))


def columns_kernel(level_ref, weight_ref, out_ref, held):
    rows, width, total = level_ref.shape
    at = lax.broadcasted_iota(jnp.int32, (width, total), 1)
    held[...] = jnp.zeros_like(held)
    for row in range(rows):
        held[row * width : (row + 1) * width] = (level_ref[row] - at).astype(jnp.float32)
        start = (rows + row) * width
        held[start : start + width] = weight_ref[row]
    turned = held[...].T
    count, levels, _ = out_ref.shape
    for k in range(count):
        out_ref[k] = turned[k * levels : (k + 1) * levels]


def join_kernel(in_ref, delta_ref, weight_ref):
    count = in_ref.shape[0]
    rows = delta_ref.shape[0]
    width = delta_ref.shape[2] // count
    for k in range(count):
        to = k * width
        for row in range(rows):
            delta_ref[row, :, to : to + width] = in_ref[k, :, row * width : (row + 1) * width]
            start = (rows + row) * width
            weight_ref[row, :, to : to + width] = in_ref[k, :, start : start + width]


def group_kernel(sums_ref, out_ref):
    near = out_ref.shape[0]
    me = lax.axis_index("lev")
    group, place = lax.div(me, near), lax.rem(me, near)
    deeper = jnp.zeros(sums_ref.shape[1:], jnp.float32)
    for k in range(sums_ref.shape[0]):
        deeper = deeper + jnp.where(k > group, sums_ref[k], 0.0)
    own = sums_ref[group]
    for k in range(near):
        out_ref[k] = deeper + jnp.where(place > k, own, 0.0)


def close_kernel(part_ref, sums_ref, out_ref):
    total = sums_ref[0]
    for k in range(1, sums_ref.shape[0]):
        total = total + sums_ref[k]
    rows, _, width = part_ref.shape
    for row in range(rows):
        out_ref[row] = part_ref[row] + total[:, row * width : (row + 1) * width]


def call(kernel, out, flops, *args, scratch=()):
    shapes = [jax.ShapeDtypeStruct(s, jnp.float32) for s in out]
    size = sum(x.size for x in args) + sum(s.size for s in shapes)
    return pl.pallas_call(
        kernel,
        out_shape=shapes,
        scratch_shapes=scratch,
        in_specs=[pl.BlockSpec(memory_space=pltpu.VMEM)] * len(args),
        out_specs=[pl.BlockSpec(memory_space=pltpu.VMEM)] * len(out),
        compiler_params=pltpu.CompilerParams(vmem_limit_bytes=16 << 20),
        cost_estimate=pl.CostEstimate(flops=flops, bytes_accessed=4 * size, transcendentals=0),
    )(*args)


def per_device(state, courant, offsets, log_thickness, surface, remap_level, remap_weight):
    count, rows, levels, width = state.shape
    lats, groups = lax.axis_size("lat"), lax.axis_size("lev")

    def swaps(n, first):
        return [p for i in range(first, n - 1, 2) for p in ((i, i + 1), (i + 1, i))]

    work = 20 * state.size
    edge = (count, 2, levels, width)
    slow, fast = pl.pallas_call(
        edges_kernel,
        out_shape=[jax.ShapeDtypeStruct((count + 1, *edge[1:]), jnp.float32)] * 2,
        in_specs=[pl.BlockSpec(memory_space=pltpu.HBM)] * 3,
        out_specs=[pl.BlockSpec(memory_space=pltpu.VMEM)] * 2,
        scratch_shapes=[pltpu.VMEM((levels, width), jnp.int32), pltpu.SemaphoreType.DMA((5,))],
        compiler_params=pltpu.CompilerParams(vmem_limit_bytes=16 << 20),
    )(*(pltpu.with_memory_space_constraint(x, pltpu.HBM) for x in (state, courant, offsets)))
    slow = lax.ppermute(slow, "lat", swaps(lats, 1))
    fast = lax.ppermute(fast, "lat", swaps(lats, 0))
    far = groups // NEAR
    close = [[j * NEAR + i for i in range(NEAR)] for j in range(far)]
    distant = [[j * NEAR + i for j in range(far)] for i in range(NEAR)]

    def exchange(x, among):
        return lax.all_to_all(x, "lev", 0, 0, tiled=True, axis_index_groups=among)

    (columns,) = call(
        columns_kernel,
        [(groups, levels, 256)],
        remap_level.size,
        jnp.transpose(remap_level, (0, 2, 1)),
        jnp.transpose(remap_weight, (0, 2, 1)),
        scratch=[pltpu.VMEM((256, remap_level.shape[1]), jnp.float32)],
    )
    columns = lax.all_to_all(columns, "lev", 0, 0, tiled=True)

    (base,) = call(east_kernel, [state.shape], work, state, courant, offsets)
    first, rest = (1, *edge[1:]), (count - 1, *edge[1:])
    field, face, slow0, slow, fast = call(
        first_kernel, [state.shape, (2, levels, width), first, rest, edge], work, base, state, slow, fast,
        courant, offsets,
    )
    slow0 = lax.ppermute(slow0, "lat", swaps(lats, 1))
    fast = lax.ppermute(fast, "lat", swaps(lats, 0))
    slow = lax.ppermute(slow, "lat", swaps(lats, 1))
    (base,) = call(east_kernel, [state.shape], work, field, courant, offsets)
    delta, weight = call(join_kernel, [log_thickness.shape] * 2, columns.size, columns)
    delta, weight = call(join_kernel, [log_thickness.shape] * 2, columns.size, columns)
    done, part, sums = call(
        heat_kernel, [log_thickness.shape, log_thickness.shape, (far, 1, rows * width)], work, base, field, slow0, fast,
        face, courant, offsets, log_thickness, surface,
    )
    (field,) = call(
        second_kernel, [state.shape], work, base, field, slow, fast, face, courant, offsets, done
    )
    sums = exchange(sums, distant)
    (sums,) = call(group_kernel, [(NEAR, 1, rows * width)], sums.size, sums)
    above = lax.ppermute(field, "lev", swaps(groups, 0))
    under = lax.ppermute(field, "lev", swaps(groups, 1))
    sums = exchange(sums, close)
    (remapped,) = call(remap_kernel, [state.shape], 2 * work, field, above, under, delta, weight)
    (geopotential,) = call(close_kernel, [log_thickness.shape], sums.size, part, sums)
    return (remapped, geopotential)


def solution(mesh):
    in_specs = (
        P(None, "lat", "lev", None),
        P(None, "lat", "lev", None),
        P(None, "lat", "lev", None),
        P("lat", "lev", None),
        P("lat", None),
        P("lat", None, "lev"),
        P("lat", None, "lev"),
    )
    out_specs = (P(None, "lat", "lev", None), P("lat", "lev", None))

    return jax.shard_map(
        per_device, mesh=mesh, in_specs=in_specs, out_specs=out_specs, check_vma=False
    )
```

```python
import jax
import jax.numpy as jnp
from jax import lax
from jax.experimental import pallas as pl
from jax.experimental.pallas import tpu as pltpu
from jax.sharding import PartitionSpec as P


NEAR = 4
EARLY = 3


def pick(offset, behind, here, ahead, beyond):
    return jnp.where(
        offset == -1,
        behind,
        jnp.where(offset == 0, here, jnp.where(offset == 1, ahead, beyond)),
    )


def east_kernel(q_ref, courant_ref, offsets_ref, base_ref):
    count, rows, levels, width = q_ref.shape
    for row in range(rows):
        offset = jnp.concatenate([offsets_ref[1, row]] * 2, axis=0)
        weight = jnp.concatenate([courant_ref[1, row]] * 2, axis=0)
        for f in range(0, count, 2):
            q = jnp.concatenate([q_ref[f, row], q_ref[f + 1, row]], axis=0)
            moved = pick(
                offset,
                pltpu.roll(q, 1, 1),
                q,
                pltpu.roll(q, width - 1, 1),
                pltpu.roll(q, width - 2, 1),
            )
            east = weight * moved
            base = q - (east - pltpu.roll(east, 1, 1))
            base_ref[f, row] = base[:levels]
            base_ref[f + 1, row] = base[levels:]


def is_even():
    return lax.rem(lax.axis_index("lat"), 2) == 0


def advected(f, base_ref, q_ref, slow_ref, fast_ref, face, courant_ref, offsets_ref, g=None):
    g = f if g is None else g
    rows = q_ref.shape[1]
    even = is_even()
    low, high = [], []
    for k in range(2):
        slow, fast = slow_ref[g, k], fast_ref[f, k]
        low.append(jnp.where(even, slow, fast))
        high.append(jnp.where(even, fast, slow))
    around = low + [q_ref[f, row] for row in range(rows)] + high
    south = face[0] * pick(face[1], *around[0:4])
    result = []
    for row in range(rows):
        north = courant_ref[0, row] * pick(offsets_ref[0, row], *around[row + 1 : row + 5])
        result.append(base_ref[f, row] - (north - south))
        south = north
    return result


def send(f, new, slow_ref, fast_ref, g=None):
    g = f if g is None else g
    even = is_even()
    for k in range(2):
        up, down = new[len(new) - 2 + k], new[k]
        slow_ref[g, k] = jnp.where(even, down, up)
        fast_ref[f, k] = jnp.where(even, up, down)


def edges_kernel(q_ref, courant_ref, offsets_ref, slow_ref, fast_ref, held, sems):
    count, rows = q_ref.shape[:2]
    even = is_even()
    up, down = rows - 2, 0
    copies = [
        pltpu.make_async_copy(
            q_ref.at[:, pl.ds(jnp.where(even, down, up), 2)], slow_ref.at[0:count], sems.at[0]
        ),
        pltpu.make_async_copy(
            q_ref.at[:, pl.ds(jnp.where(even, up, down), 2)], fast_ref.at[0:count], sems.at[1]
        ),
        pltpu.make_async_copy(courant_ref.at[0, rows - 1], slow_ref.at[count, 0], sems.at[2]),
        pltpu.make_async_copy(courant_ref.at[0, rows - 1], fast_ref.at[count, 0], sems.at[3]),
        pltpu.make_async_copy(offsets_ref.at[0, rows - 1], held, sems.at[4]),
    ]
    for copy in copies:
        copy.start()
    copies[4].wait()
    offset = held[...].astype(jnp.float32)
    slow_ref[count, 1] = offset
    fast_ref[count, 1] = offset
    for copy in copies[:4]:
        copy.wait()


def first_kernel(
    base_ref, q_ref, slow_ref, fast_ref, courant_ref, offsets_ref, out_ref, face_ref, slow0_ref, next_slow_ref,
    next_fast_ref,
):
    count, rows = q_ref.shape[:2]
    face = [jnp.where(is_even(), slow_ref[count, k], fast_ref[count, k]) for k in range(2)]
    for k in range(2):
        face_ref[k] = face[k]
    face[1] = face[1].astype(jnp.int32)
    for f in range(count):
        new = advected(f, base_ref, q_ref, slow_ref, fast_ref, face, courant_ref, offsets_ref)
        for row in range(rows):
            out_ref[f, row] = new[row]
        if f < EARLY:
            send(f, new, slow0_ref, next_fast_ref)
        else:
            send(f, new, next_slow_ref, next_fast_ref, f - EARLY)


def heat(new, thickness_ref, surface_ref, part_ref, sums_ref):
    sums = []
    for row, value in enumerate(new):
        levels = value.shape[0]
        heating = value * thickness_ref[row]
        below = jnp.concatenate([heating, jnp.zeros_like(heating)], axis=0)
        step = 1
        while step < levels:
            below = below + pltpu.roll(below, 2 * levels - step, 0)
            step *= 2
        part_ref[row] = below[:levels] - 0.5 * heating + surface_ref[row : row + 1]
        sums.append(below[0:1])
    sums = jnp.concatenate(sums, axis=1)
    for k in range(sums_ref.shape[0]):
        sums_ref[k] = sums


def heat_kernel(
    base_ref, q_ref, slow_ref, fast_ref, face_ref, courant_ref, offsets_ref, thickness_ref, surface_ref,
    out_ref, part_ref, sums_ref,
):
    face = face_ref[0], face_ref[1].astype(jnp.int32)
    new = advected(0, base_ref, q_ref, slow_ref, fast_ref, face, courant_ref, offsets_ref)
    for row, value in enumerate(new):
        out_ref[row] = value
    heat(new, thickness_ref, surface_ref, part_ref, sums_ref)


def second_kernel(
    base_ref, q_ref, early_ref, slow_ref, fast_ref, face_ref, courant_ref, offsets_ref, done_ref, out_ref
):
    count, rows = q_ref.shape[:2]
    face = face_ref[0], face_ref[1].astype(jnp.int32)
    for row in range(rows):
        out_ref[0, row] = done_ref[row]
    for f in range(1, count):
        halo_ref, g = (early_ref, f) if f < EARLY else (slow_ref, f - EARLY)
        new = advected(f, base_ref, q_ref, halo_ref, fast_ref, face, courant_ref, offsets_ref, g)
        for row in range(rows):
            out_ref[f, row] = new[row]


def remap_kernel(q_ref, chip_ref, other_ref, delta_ref, weight_ref, out_ref):
    count, rows, levels, width = q_ref.shape
    me, last = lax.axis_index("lev"), lax.axis_size("lev") - 1
    even = lax.rem(me, 2) == 0

    def body(above_ref, under_ref):
        sub = lax.broadcasted_iota(jnp.int32, (8, width), 0)
        for row in range(rows):
            delta = delta_ref[row].astype(jnp.int32)
            source = jnp.concatenate([delta, delta], axis=0) + (sub & 3) + 2
            t = weight_ref[row]
            for f in range(count):
                own = q_ref[f, row]
                if above_ref is None:
                    above = jnp.broadcast_to(own[0:1], own.shape)
                else:
                    above = above_ref[f, row]
                if under_ref is None:
                    under = jnp.broadcast_to(own[levels - 1 :], own.shape)
                else:
                    under = under_ref[f, row]
                early = jnp.concatenate([above, own], axis=0)
                late = jnp.concatenate([own, under], axis=0)
                windows = [early]
                for k in range(1, 4):
                    windows.append(
                        jnp.where(sub < 4, pltpu.roll(early, 8 - k, 0), pltpu.roll(late, 4 - k, 0))
                    )
                windows.append(late)
                w0, w1, w2, w3, w4 = windows
                left = 7.0 * (w1 + w2) - (w0 + w3)
                right = 7.0 * (w2 + w3) - (w1 + w4)
                slope = right - left
                curve = 6.0 * w2 - 0.25 * (left + right)
                left, slope, curve = (
                    jnp.take_along_axis(x, source, axis=0)[:levels] for x in (left, slope, curve)
                )
                out_ref[f, row] = (left + t * slope) * (1.0 / 12.0) + t * (1.0 - t) * curve

    pl.when(even & (me > 0))(lambda: body(other_ref, chip_ref))
    pl.when(~even & (me < last))(lambda: body(chip_ref, other_ref))
    pl.when(me == 0)(lambda: body(None, chip_ref))
    pl.when(me == last)(lambda: body(chip_ref, None))


def columns_kernel(level_ref, weight_ref, out_ref, held):
    rows, width, total = level_ref.shape
    at = lax.broadcasted_iota(jnp.int32, (width, total), 1)
    held[...] = jnp.zeros_like(held)
    for row in range(rows):
        held[row * width : (row + 1) * width] = (level_ref[row] - at).astype(jnp.float32)
        start = (rows + row) * width
        held[start : start + width] = weight_ref[row]
    turned = held[...].T
    count, levels, _ = out_ref.shape
    for k in range(count):
        out_ref[k] = turned[k * levels : (k + 1) * levels]


def join_kernel(in_ref, delta_ref, weight_ref):
    count = in_ref.shape[0]
    rows = delta_ref.shape[0]
    width = delta_ref.shape[2] // count
    for k in range(count):
        to = k * width
        for row in range(rows):
            delta_ref[row, :, to : to + width] = in_ref[k, :, row * width : (row + 1) * width]
            start = (rows + row) * width
            weight_ref[row, :, to : to + width] = in_ref[k, :, start : start + width]


def group_kernel(sums_ref, out_ref):
    near = out_ref.shape[0]
    me = lax.axis_index("lev")
    group, place = lax.div(me, near), lax.rem(me, near)
    deeper = jnp.zeros(sums_ref.shape[1:], jnp.float32)
    for k in range(sums_ref.shape[0]):
        deeper = deeper + jnp.where(k > group, sums_ref[k], 0.0)
    own = sums_ref[group]
    for k in range(near):
        out_ref[k] = deeper + jnp.where(place > k, own, 0.0)


def close_kernel(part_ref, sums_ref, out_ref):
    total = sums_ref[0]
    for k in range(1, sums_ref.shape[0]):
        total = total + sums_ref[k]
    rows, _, width = part_ref.shape
    for row in range(rows):
        out_ref[row] = part_ref[row] + total[:, row * width : (row + 1) * width]


def call(kernel, out, flops, *args, scratch=()):
    shapes = [jax.ShapeDtypeStruct(s, jnp.float32) for s in out]
    size = sum(x.size for x in args) + sum(s.size for s in shapes)
    return pl.pallas_call(
        kernel,
        out_shape=shapes,
        scratch_shapes=scratch,
        in_specs=[pl.BlockSpec(memory_space=pltpu.VMEM)] * len(args),
        out_specs=[pl.BlockSpec(memory_space=pltpu.VMEM)] * len(out),
        compiler_params=pltpu.CompilerParams(vmem_limit_bytes=16 << 20),
        cost_estimate=pl.CostEstimate(flops=flops, bytes_accessed=4 * size, transcendentals=0),
    )(*args)


def per_device(state, courant, offsets, log_thickness, surface, remap_level, remap_weight):
    count, rows, levels, width = state.shape
    lats, groups = lax.axis_size("lat"), lax.axis_size("lev")

    def swaps(n, first):
        return [p for i in range(first, n - 1, 2) for p in ((i, i + 1), (i + 1, i))]

    work = 20 * state.size
    edge = (count, 2, levels, width)
    slow, fast = pl.pallas_call(
        edges_kernel,
        out_shape=[jax.ShapeDtypeStruct((count + 1, *edge[1:]), jnp.float32)] * 2,
        in_specs=[pl.BlockSpec(memory_space=pltpu.HBM)] * 3,
        out_specs=[pl.BlockSpec(memory_space=pltpu.VMEM)] * 2,
        scratch_shapes=[pltpu.VMEM((levels, width), jnp.int32), pltpu.SemaphoreType.DMA((5,))],
        compiler_params=pltpu.CompilerParams(vmem_limit_bytes=16 << 20),
    )(*(pltpu.with_memory_space_constraint(x, pltpu.HBM) for x in (state, courant, offsets)))
    slow = lax.ppermute(slow, "lat", swaps(lats, 1))
    fast = lax.ppermute(fast, "lat", swaps(lats, 0))
    far = groups // NEAR
    close = [[j * NEAR + i for i in range(NEAR)] for j in range(far)]
    distant = [[j * NEAR + i for j in range(far)] for i in range(NEAR)]

    def exchange(x, among):
        return lax.all_to_all(x, "lev", 0, 0, tiled=True, axis_index_groups=among)

    (columns,) = call(
        columns_kernel,
        [(groups, levels, 256)],
        remap_level.size,
        jnp.transpose(remap_level, (0, 2, 1)),
        jnp.transpose(remap_weight, (0, 2, 1)),
        scratch=[pltpu.VMEM((256, remap_level.shape[1]), jnp.float32)],
    )
    columns = lax.all_to_all(columns, "lev", 0, 0, tiled=True)

    (base,) = call(east_kernel, [state.shape], work, state, courant, offsets)
    first, rest = (EARLY, *edge[1:]), (count - EARLY, *edge[1:])
    field, face, slow0, slow, fast = call(
        first_kernel, [state.shape, (2, levels, width), first, rest, edge], work, base, state, slow, fast,
        courant, offsets,
    )
    slow0 = lax.ppermute(slow0, "lat", swaps(lats, 1))
    fast = lax.ppermute(fast, "lat", swaps(lats, 0))
    slow = lax.ppermute(slow, "lat", swaps(lats, 1))
    (base,) = call(east_kernel, [state.shape], work, field, courant, offsets)
    delta, weight = call(join_kernel, [log_thickness.shape] * 2, columns.size, columns)
    delta, weight = call(join_kernel, [log_thickness.shape] * 2, columns.size, columns)
    done, part, sums = call(
        heat_kernel, [log_thickness.shape, log_thickness.shape, (far, 1, rows * width)], work, base, field, slow0, fast,
        face, courant, offsets, log_thickness, surface,
    )
    (field,) = call(
        second_kernel, [state.shape], work, base, field, slow0, slow, fast, face, courant, offsets, done
    )
    sums = exchange(sums, distant)
    (sums,) = call(group_kernel, [(NEAR, 1, rows * width)], sums.size, sums)
    above = lax.ppermute(field, "lev", swaps(groups, 0))
    under = lax.ppermute(field, "lev", swaps(groups, 1))
    sums = exchange(sums, close)
    (remapped,) = call(
        remap_kernel, [state.shape], 2 * work, field, above, under, delta, weight
    )
    (geopotential,) = call(close_kernel, [log_thickness.shape], sums.size, part, sums)
    return (remapped, geopotential)


def solution(mesh):
    in_specs = (
        P(None, "lat", "lev", None),
        P(None, "lat", "lev", None),
        P(None, "lat", "lev", None),
        P("lat", "lev", None),
        P("lat", None),
        P("lat", None, "lev"),
        P("lat", None, "lev"),
    )
    out_specs = (P(None, "lat", "lev", None), P("lat", "lev", None))

    return jax.shard_map(per_device, mesh=mesh, in_specs=in_specs, out_specs=out_specs, check_vma=False)
```
